32 devices in a mesh: groups: 2 (over y), sub: 16 (over z, x, core).
Axes of the slice: x: 2, y: 2, z: 4, core: 2. Of those that a mesh axis runs over, the one named last changes fastest.
Arguments:
- samples: bfloat16 [16896, 512], P(('groups', 'sub')), parts along dimension 0, may hold values from -6 to 6
- channel_order: int32 [512], replicated, may hold values from 0 to 511, each once
- merge_table: int32 [9, 3, 256], replicated, may hold values from 0 to 128, as said below
Outputs:
- spectra: float32 [512, 4096], P(('groups', 'sub')), parts along dimension 0
The draws below stay inside these ranges and needn't reach their ends.
There are 2 independent parts, one for each index of `groups`. The reference program is written for one: setup_inputs(seed, part) draws one part's arguments, and reference() takes and returns one part's arrays. A program takes and returns all parts, laid end to end along the dimension named above; an argument that names none is the same for every part. Nothing has to cross between parts.
Inputs may be any that keep to these rules, and one draw needn't show every extreme that they name: `channel_order`: a permutation of the 512 channels. `merge_table`: for level l, entry j is row d = j % 2**(l-1) of merged subband j // 2**(l-1); with C = max(1, 2**(l-2)) and e = 8, entries 0 and 1 lie in [e * (d // (2 e)), e * (d // (2 e)) + min(C, e)), and entry 2 equals entry 0 or entry 0 plus 1.
All inputs are finite; a program needn't handle non-finite values.
Results may differ from the reference program's by a relative error of at most 0.012.
Values may be sent and summed in bfloat16 or wider, within the bound.
A program may use at most 64 MiB of HBM per device.

```python
import math
import jax
import jax.numpy as jnp
from jax import lax

CH_DEV = 32
CROSS = 4
CHANNELS = 512
LEVELS = 9
DMAX = 256
SAMPLES = 8192
SPAN = 8448
N_SUB = 16


def draw_merge_table(key, part):
    quarter = CH_DEV // 4
    owned_rows = CH_DEV // 2
    stacked = []
    for level_num in range(1, LEVELS + 1):
        span_rows = 2 ** (level_num - 1)
        child_rows = max(1, 2 ** (level_num - 2))
        choices_wide = min(child_rows, quarter)
        entry_index = jnp.arange(DMAX, dtype=jnp.int32)
        row_base = entry_index % span_rows // owned_rows * quarter
        key_lower, key_upper, key_shift = jax.random.split(jax.random.fold_in(key, 7919 + level_num), 3)
        lower_rows = row_base + jax.random.randint(key_lower, (DMAX,), 0, choices_wide, dtype=jnp.int32)
        upper_rows = row_base + jax.random.randint(key_upper, (DMAX,), 0, choices_wide, dtype=jnp.int32)
        shifts = lower_rows + jax.random.randint(key_shift, (DMAX,), 0, 2, dtype=jnp.int32)
        stacked.append(jnp.stack([lower_rows, upper_rows, shifts], axis=0))
    return jnp.stack(stacked, axis=0)


def levels(key, extent, pieces, least, high):
    level = 1.0
    for axis_at, blocks in pieces:
        draws = jax.random.uniform(jax.random.fold_in(jax.random.fold_in(key, 6), axis_at), (blocks,), jnp.float32, least / len(pieces), high / len(pieces))
        level = level * jnp.repeat(jnp.exp(draws), extent[axis_at] // blocks).reshape((-1,) + (1,) * (len(extent) - 1 - axis_at))
    return level


def bell_draw(key, dims, deviation, most, cuts=(), kind=jnp.bfloat16):
    result = deviation * jax.random.normal(key, dims, jnp.float32)
    if cuts:
        result = result * levels(key, dims, cuts, -0.22, 0.18)
    return jnp.clip(result, -most, most).astype(kind)


def setup_inputs(seed: int = 0, part: int = 0) -> dict:
    streams_of = jax.random.split(jax.random.key(seed), 4)
    part_keys = jax.random.split(jax.random.fold_in(streams_of[3], part), 4)
    samples = bell_draw(part_keys[0], (SPAN, CHANNELS), 1.0, 6.0, ((0, 16),))
    channel_order = jax.random.permutation(streams_of[1], CHANNELS).astype(jnp.int32)
    merge_table = draw_merge_table(jax.random.fold_in(streams_of[3], 71), part)
    return dict(samples=samples, channel_order=channel_order, merge_table=merge_table)


def delay_rows(values, shifts, margin, time_axis):
    length = values.shape[time_axis]
    if time_axis == 1:
        padded = jnp.pad(values, ((0, 0), (0, margin)))
        return jax.vmap(lambda series, offset: lax.dynamic_slice_in_dim(series, offset, length))(padded, shifts)
    padded = jnp.pad(values, ((0, margin), (0, 0)))
    return jax.vmap(lambda series, offset: lax.dynamic_slice_in_dim(series, offset, length), in_axes=(1, 0), out_axes=1)(padded, shifts)


def merge_level(current, entries, child_rows, span_rows, time_axis):
    outputs = jnp.arange(entries.shape[1], dtype=jnp.int32)
    starts = 2 * child_rows * (outputs // span_rows)
    lower_rows = jnp.take(current, starts + entries[0], axis=1 - time_axis)
    upper_rows = jnp.take(current, starts + child_rows + entries[1], axis=1 - time_axis)
    moved_rows = delay_rows(upper_rows, entries[2], child_rows, time_axis)
    return (lower_rows.astype(jnp.float32) + moved_rows.astype(jnp.float32)).astype(jnp.bfloat16)


def spectrum(delays, channels):
    row_count = delays.shape[0]
    length = delays.shape[1]
    fold_size = length // 128
    first_index = jnp.arange(fold_size, dtype=jnp.int32)
    lane_index = jnp.arange(128, dtype=jnp.int32)
    half_index = jnp.arange(64, dtype=jnp.int32)
    angle_one = (2.0 * math.pi / fold_size) * ((first_index[:, None] * first_index[None, :]) % fold_size).astype(jnp.float32)
    cos_one = jnp.cos(angle_one).astype(jnp.bfloat16).astype(jnp.float32)
    sin_one = jnp.sin(angle_one).astype(jnp.bfloat16).astype(jnp.float32)
    angle_two = (2.0 * math.pi / length) * ((first_index[:, None] * lane_index[None, :]) % length).astype(jnp.float32)
    twist_cos = jnp.cos(angle_two)
    twist_sin = jnp.sin(angle_two)
    angle_three = (2.0 * math.pi / 128) * ((lane_index[:, None] * half_index[None, :]) % 128).astype(jnp.float32)
    cos_three = jnp.cos(angle_three).astype(jnp.bfloat16).astype(jnp.float32)
    sin_three = jnp.sin(angle_three).astype(jnp.bfloat16).astype(jnp.float32)
    series = delays.reshape(row_count, fold_size, 128).astype(jnp.float32)
    highest = lax.Precision.HIGHEST
    first_re = jnp.einsum("kn,rnm->rkm", cos_one, series, precision=highest)
    first_im = -jnp.einsum("kn,rnm->rkm", sin_one, series, precision=highest)
    twisted_re = (first_re * twist_cos + first_im * twist_sin).astype(jnp.bfloat16).astype(jnp.float32)
    twisted_im = (first_im * twist_cos - first_re * twist_sin).astype(jnp.bfloat16).astype(jnp.float32)
    out_re = jnp.einsum("rkn,nj->rjk", twisted_re, cos_three, precision=highest) + jnp.einsum("rkn,nj->rjk", twisted_im, sin_three, precision=highest)
    out_im = jnp.einsum("rkn,nj->rjk", twisted_im, cos_three, precision=highest) - jnp.einsum("rkn,nj->rjk", twisted_re, sin_three, precision=highest)
    power = (out_re * out_re + out_im * out_im) / (length * channels)
    return power.reshape(row_count, 64 * fold_size)


def reference(samples, channel_order, merge_table):
    current = jnp.take(samples, channel_order, axis=1).T
    for level_num in range(1, LEVELS + 1):
        current = merge_level(current, merge_table[level_num - 1], max(1, 2 ** (level_num - 2)), 2 ** (level_num - 1), 1)
    owned_rows = CH_DEV // 2
    reversal = []
    for position in range(N_SUB):
        flipped = 0
        for bit_num in range(CROSS):
            flipped = flipped | (((position >> bit_num) & 1) << (CROSS - 1 - bit_num))
        reversal.append(flipped)
    blocks = current.reshape(N_SUB, owned_rows, SPAN)
    blocks = jnp.take(blocks, jnp.array(reversal, dtype=jnp.int32), axis=0).reshape(DMAX, SPAN)
    return spectrum(blocks[:, :SAMPLES], CHANNELS)
```

```python
import functools
import math

import jax
import jax.numpy as jnp
from jax import lax
from jax.experimental import pallas as pl
from jax.experimental.pallas import tpu as pltpu
from jax.sharding import PartitionSpec as P

LOCAL = 5
CH_DEV = 32
SAMPLES = 8192


def from_partner(block, axis, apart):
    count = lax.axis_size(axis)
    route = []
    for low in range(count):
        high = low | 1 << apart
        if high != low and high < count:
            route += [(low, high), (high, low)]
    return lax.ppermute(block, axis, route)


def delay_rows(values, shifts, margin, time_axis):
    length = values.shape[time_axis]
    moved = values
    for bit_num in range(max(1, margin.bit_length())):
        offset = 2**bit_num
        rolled = jnp.pad(moved[:, offset:], ((0, 0), (0, offset)))
        flagged = shifts >> bit_num & 1 == 1
        flagged = flagged[:, None]
        moved = jnp.where(flagged, rolled, moved)
    return moved


def merge_level(current, entries, child_rows, span_rows, time_axis):
    outputs = jnp.arange(entries.shape[1], dtype=jnp.int32)
    starts = 2 * child_rows * (outputs // span_rows)
    lower_rows = jnp.take(current, starts + entries[0], axis=1 - time_axis)
    upper_rows = jnp.take(current, starts + child_rows + entries[1], axis=1 - time_axis)
    moved_rows = delay_rows(upper_rows, entries[2], child_rows, time_axis)
    return (lower_rows.astype(jnp.float32) + moved_rows.astype(jnp.float32)).astype(jnp.bfloat16)


def spectrum(delays, channels):
    row_count = delays.shape[0]
    length = delays.shape[1]
    fold_size = length // 128
    first_index = jnp.arange(fold_size, dtype=jnp.int32)
    lane_index = jnp.arange(128, dtype=jnp.int32)
    half_index = jnp.arange(64, dtype=jnp.int32)
    angle_one = (
        2.0
        * math.pi
        / fold_size
        * (first_index[:, None] * first_index[None, :] % fold_size).astype(jnp.float32)
    )
    cos_one = jnp.cos(angle_one).astype(jnp.bfloat16)
    sin_one = jnp.sin(angle_one).astype(jnp.bfloat16)
    angle_two = (
        2.0
        * math.pi
        / length
        * (first_index[:, None] * lane_index[None, :] % length).astype(jnp.float32)
    )
    twist_cos = jnp.cos(angle_two)
    twist_sin = jnp.sin(angle_two)
    angle_three = (
        2.0 * math.pi / 128 * (lane_index[:, None] * half_index[None, :] % 128).astype(jnp.float32)
    )
    cos_three = jnp.cos(angle_three).astype(jnp.bfloat16)
    sin_three = jnp.sin(angle_three).astype(jnp.bfloat16)
    series = delays.reshape(row_count, fold_size, 128)
    first_re = jnp.einsum("kn,rnm->rkm", cos_one, series, preferred_element_type=jnp.float32)
    first_im = -jnp.einsum("kn,rnm->rkm", sin_one, series, preferred_element_type=jnp.float32)
    twisted_re = (first_re * twist_cos + first_im * twist_sin).astype(jnp.bfloat16)
    twisted_im = (first_im * twist_cos - first_re * twist_sin).astype(jnp.bfloat16)
    out_re = jnp.einsum(
        "rkn,nj->rjk", twisted_re, cos_three, preferred_element_type=jnp.float32
    ) + jnp.einsum("rkn,nj->rjk", twisted_im, sin_three, preferred_element_type=jnp.float32)
    out_im = jnp.einsum(
        "rkn,nj->rjk", twisted_im, cos_three, preferred_element_type=jnp.float32
    ) - jnp.einsum("rkn,nj->rjk", twisted_re, sin_three, preferred_element_type=jnp.float32)
    power = (out_re * out_re + out_im * out_im) / (length * channels)
    return power.reshape(row_count, 64 * fold_size)


def local(samples, channel_order, merge_table):
    owners = lax.axis_size("sub")
    owner_index = lax.axis_index("sub")
    owned_rows = CH_DEV // 2
    quarter = CH_DEV // 4
    window = samples.shape[0]
    channels = samples.shape[1]
    ordered = jnp.take(samples, channel_order, axis=1).T.reshape(owners, CH_DEV, window)
    current = lax.all_to_all(ordered, "sub", split_axis=0, concat_axis=2, tiled=True).reshape(
        CH_DEV, window * owners
    )
    for level_num in range(1, LOCAL + 1):
        entries = lax.dynamic_slice_in_dim(
            merge_table[level_num - 1], owner_index * owned_rows, owned_rows, 1
        )
        current = merge_level(
            current, entries, max(1, 2 ** (level_num - 2)), 2 ** (level_num - 1), 1
        )
    block_index = jnp.zeros((), jnp.int32)
    for bit_num in range(owners.bit_length() - 1):
        level_num = LOCAL + bit_num + 1
        half_bit = owner_index >> bit_num & 1
        block_index = block_index * 2 + half_bit
        span_rows = owned_rows * 2 ** (bit_num + 1)
        child_rows = span_rows // 2
        subband = owner_index >> bit_num + 1
        entries = lax.dynamic_slice_in_dim(
            merge_table[level_num - 1],
            subband * span_rows + owned_rows * block_index,
            owned_rows,
            1,
        )
        kept_rows = lax.dynamic_slice_in_dim(current, half_bit * quarter, quarter, 0)
        sent_rows = lax.dynamic_slice_in_dim(current, (1 - half_bit) * quarter, quarter, 0)
        partner = from_partner(sent_rows, "sub", bit_num)
        row_base = quarter * block_index
        is_low = half_bit == 0
        lower_part = jnp.where(is_low, kept_rows, partner)
        upper_part = jnp.where(is_low, partner, kept_rows)
        lower_rows = jnp.take(lower_part, entries[0] - row_base, axis=0)
        upper_rows = jnp.take(upper_part, entries[1] - row_base, axis=0)
        moved_rows = delay_rows(upper_rows, entries[2], child_rows, 1)
        current = (lower_rows.astype(jnp.float32) + moved_rows.astype(jnp.float32)).astype(
            jnp.bfloat16
        )
    return spectrum(current[:, :SAMPLES], channels)


def reversed_bits(values, bits):
    flipped = jnp.zeros_like(values)
    for bit_num in range(bits):
        flipped = flipped | ((values >> bit_num & 1) << (bits - 1 - bit_num))
    return flipped


def one_hot(row_index, depth):
    rows = lax.broadcasted_iota(jnp.int32, (depth, row_index.shape[1]), 0)
    return (rows == row_index).astype(jnp.float32).astype(jnp.bfloat16)


def merge_kernel(owners, step, order_ref, table_ref, before_ref, own_ref, after_ref, out_ref, joined, current):
    levels, _, rows = table_ref.shape
    extra = before_ref.shape[0]
    window = own_ref.shape[0]
    length = out_ref.shape[1]
    whole = length + rows
    joined[0:extra, :] = before_ref[...]
    joined[extra : extra + window, :] = own_ref[...]
    joined[extra + window :, :] = after_ref[...]
    first = pl.multiple_of(extra - step * lax.axis_index("sub"), step)
    lanes = lax.broadcasted_iota(jnp.int32, (1, rows), 1)
    have = whole
    left = rows
    for level_num in range(1, levels + 1):
        child_rows = max(1, 2 ** (level_num - 2))
        entries = table_ref[level_num - 1]
        shifts = entries[2:3]
        if level_num == 1:
            chosen = one_hot(order_ref[...], order_ref.shape[1])
            source = joined[pl.ds(first, whole), :]
        else:
            starts = 2 * child_rows * (lanes >> (level_num - 1))
            lower = one_hot(starts + entries[0:1], rows)
            upper = one_hot(starts + child_rows + entries[1:2], rows)
            chosen = jnp.concatenate([lower, upper], axis=1)
            source = current[0:have, :]
        left -= child_rows
        keep = -(-(length + left) // 16) * 16
        picked = jnp.dot(source, chosen, preferred_element_type=jnp.float32)
        for base in range(0, rows, 128):
            moved = picked[:, rows + base : rows + base + 128]
            amounts = shifts[:, base : base + 128]
            for bit_num in reversed(range(child_rows.bit_length())):
                size = moved.shape[0]
                rolled = pltpu.roll(moved, size - 2**bit_num, axis=0)
                flagged = jnp.broadcast_to(amounts >> bit_num & 1, moved.shape) == 1
                moved = jnp.where(flagged, rolled, moved)
                needed = min(size, keep + -(-(2**bit_num - 1) // 8) * 8)
                moved = moved[0:needed]
            current[0:keep, base : base + 128] = (
                picked[0:keep, base : base + 128] + moved[0:keep]
            ).astype(jnp.bfloat16)
        have = keep
    held = rows // owners
    places = lax.broadcasted_iota(jnp.int32, (rows, rows), 0)
    shift = held.bit_length() - 1
    sources = (reversed_bits(places >> shift, owners.bit_length() - 1) << shift) + (places & (held - 1))
    turned = (lax.broadcasted_iota(jnp.int32, (rows, rows), 1) == sources).astype(jnp.float32)
    out_ref[...] = lax.dot_general(
        turned.astype(jnp.bfloat16),
        current[0:length, :],
        (((1,), (1,)), ((), ())),
        preferred_element_type=jnp.float32,
    ).astype(jnp.bfloat16)


def local_sliced(samples, channel_order, merge_table):
    owners = lax.axis_size("sub")
    window, channels = samples.shape
    rows = merge_table.shape[2]
    length = window - rows // owners
    step = window - length
    extra = step * (owners - 1)
    onward = [(at, at + 1) for at in range(owners - 1)]
    back = [(at + 1, at) for at in range(owners - 1)]
    before = lax.ppermute(samples[window - extra :], "sub", onward)
    after = lax.ppermute(samples[:extra], "sub", back)
    order = channel_order.reshape(rows, 2).T.reshape(1, channels)
    vmem = pl.BlockSpec(memory_space=pltpu.VMEM)
    delays = pl.pallas_call(
        functools.partial(merge_kernel, owners, step),
        out_shape=jax.ShapeDtypeStruct((rows, length), jnp.bfloat16),
        in_specs=[vmem] * 5,
        out_specs=vmem,
        scratch_shapes=[
            pltpu.VMEM((window + 2 * extra, channels), jnp.bfloat16),
            pltpu.VMEM((length + rows, rows), jnp.bfloat16),
        ],
        compiler_params=pltpu.CompilerParams(vmem_limit_bytes=32 * 1024 * 1024),
        name="merge_rows",
    )(order, merge_table, before, samples, after)
    held = rows // owners
    blocks = lax.all_to_all(delays.reshape(owners, held, length), "sub", 0, 0, tiled=True)
    series = blocks.transpose(1, 0, 2).reshape(held, owners * length)
    return spectrum(series, channels)


def is_sliced(window, owners, rows):
    step = rows // owners
    length = window - step
    return step % 16 == 0 and length % 128 == 0 and step * (owners - 1) <= window


def local_any(samples, channel_order, merge_table):
    if is_sliced(samples.shape[0], lax.axis_size("sub"), merge_table.shape[2]):
        return local_sliced(samples, channel_order, merge_table)
    return local(samples, channel_order, merge_table)


def solution(mesh):
    in_specs = (P(("groups", "sub"), None), P(), P())
    out_specs = P(("groups", "sub"), None)
    return jax.shard_map(local_any, mesh=mesh, in_specs=in_specs, out_specs=out_specs, check_vma=False)
```

```python
import functools
import math

import jax
import jax.numpy as jnp
from jax import lax
from jax.experimental import pallas as pl
from jax.experimental.pallas import tpu as pltpu
from jax.sharding import PartitionSpec as P

LOCAL = 5
MESH = pl.DeviceIdType.MESH
CH_DEV = 32
SAMPLES = 8192


def from_partner(block, axis, apart):
    count = lax.axis_size(axis)
    route = []
    for low in range(count):
        high = low | 1 << apart
        if high != low and high < count:
            route += [(low, high), (high, low)]
    return lax.ppermute(block, axis, route)


def delay_rows(values, shifts, margin, time_axis):
    length = values.shape[time_axis]
    moved = values
    for bit_num in range(max(1, margin.bit_length())):
        offset = 2**bit_num
        rolled = jnp.pad(moved[:, offset:], ((0, 0), (0, offset)))
        flagged = shifts >> bit_num & 1 == 1
        flagged = flagged[:, None]
        moved = jnp.where(flagged, rolled, moved)
    return moved


def merge_level(current, entries, child_rows, span_rows, time_axis):
    outputs = jnp.arange(entries.shape[1], dtype=jnp.int32)
    starts = 2 * child_rows * (outputs // span_rows)
    lower_rows = jnp.take(current, starts + entries[0], axis=1 - time_axis)
    upper_rows = jnp.take(current, starts + child_rows + entries[1], axis=1 - time_axis)
    moved_rows = delay_rows(upper_rows, entries[2], child_rows, time_axis)
    return (lower_rows.astype(jnp.float32) + moved_rows.astype(jnp.float32)).astype(jnp.bfloat16)


def spectrum(delays, channels):
    row_count = delays.shape[0]
    length = delays.shape[1]
    fold_size = length // 128
    first_index = jnp.arange(fold_size, dtype=jnp.int32)
    lane_index = jnp.arange(128, dtype=jnp.int32)
    half_index = jnp.arange(64, dtype=jnp.int32)
    angle_one = (
        2.0
        * math.pi
        / fold_size
        * (first_index[:, None] * first_index[None, :] % fold_size).astype(jnp.float32)
    )
    cos_one = jnp.cos(angle_one).astype(jnp.bfloat16)
    sin_one = jnp.sin(angle_one).astype(jnp.bfloat16)
    angle_two = (
        2.0
        * math.pi
        / length
        * (first_index[:, None] * lane_index[None, :] % length).astype(jnp.float32)
    )
    twist_cos = jnp.cos(angle_two)
    twist_sin = jnp.sin(angle_two)
    angle_three = (
        2.0 * math.pi / 128 * (lane_index[:, None] * half_index[None, :] % 128).astype(jnp.float32)
    )
    cos_three = jnp.cos(angle_three).astype(jnp.bfloat16)
    sin_three = jnp.sin(angle_three).astype(jnp.bfloat16)
    series = delays.reshape(row_count, fold_size, 128)
    first_re = jnp.einsum("kn,rnm->rkm", cos_one, series, preferred_element_type=jnp.float32)
    first_im = -jnp.einsum("kn,rnm->rkm", sin_one, series, preferred_element_type=jnp.float32)
    twisted_re = (first_re * twist_cos + first_im * twist_sin).astype(jnp.bfloat16)
    twisted_im = (first_im * twist_cos - first_re * twist_sin).astype(jnp.bfloat16)
    out_re = jnp.einsum(
        "rkn,nj->rjk", twisted_re, cos_three, preferred_element_type=jnp.float32
    ) + jnp.einsum("rkn,nj->rjk", twisted_im, sin_three, preferred_element_type=jnp.float32)
    out_im = jnp.einsum(
        "rkn,nj->rjk", twisted_im, cos_three, preferred_element_type=jnp.float32
    ) - jnp.einsum("rkn,nj->rjk", twisted_re, sin_three, preferred_element_type=jnp.float32)
    power = (out_re * out_re + out_im * out_im) / (length * channels)
    return power.reshape(row_count, 64 * fold_size)


def local(samples, channel_order, merge_table):
    owners = lax.axis_size("sub")
    owner_index = lax.axis_index("sub")
    owned_rows = CH_DEV // 2
    quarter = CH_DEV // 4
    window = samples.shape[0]
    channels = samples.shape[1]
    ordered = jnp.take(samples, channel_order, axis=1).T.reshape(owners, CH_DEV, window)
    current = lax.all_to_all(ordered, "sub", split_axis=0, concat_axis=2, tiled=True).reshape(
        CH_DEV, window * owners
    )
    for level_num in range(1, LOCAL + 1):
        entries = lax.dynamic_slice_in_dim(
            merge_table[level_num - 1], owner_index * owned_rows, owned_rows, 1
        )
        current = merge_level(
            current, entries, max(1, 2 ** (level_num - 2)), 2 ** (level_num - 1), 1
        )
    block_index = jnp.zeros((), jnp.int32)
    for bit_num in range(owners.bit_length() - 1):
        level_num = LOCAL + bit_num + 1
        half_bit = owner_index >> bit_num & 1
        block_index = block_index * 2 + half_bit
        span_rows = owned_rows * 2 ** (bit_num + 1)
        child_rows = span_rows // 2
        subband = owner_index >> bit_num + 1
        entries = lax.dynamic_slice_in_dim(
            merge_table[level_num - 1],
            subband * span_rows + owned_rows * block_index,
            owned_rows,
            1,
        )
        kept_rows = lax.dynamic_slice_in_dim(current, half_bit * quarter, quarter, 0)
        sent_rows = lax.dynamic_slice_in_dim(current, (1 - half_bit) * quarter, quarter, 0)
        partner = from_partner(sent_rows, "sub", bit_num)
        row_base = quarter * block_index
        is_low = half_bit == 0
        lower_part = jnp.where(is_low, kept_rows, partner)
        upper_part = jnp.where(is_low, partner, kept_rows)
        lower_rows = jnp.take(lower_part, entries[0] - row_base, axis=0)
        upper_rows = jnp.take(upper_part, entries[1] - row_base, axis=0)
        moved_rows = delay_rows(upper_rows, entries[2], child_rows, 1)
        current = (lower_rows.astype(jnp.float32) + moved_rows.astype(jnp.float32)).astype(
            jnp.bfloat16
        )
    return spectrum(current[:, :SAMPLES], channels)


def reversed_bits(values, bits):
    flipped = jnp.zeros_like(values)
    for bit_num in range(bits):
        flipped = flipped | ((values >> bit_num & 1) << (bits - 1 - bit_num))
    return flipped


def one_hot(row_index, depth):
    rows = lax.broadcasted_iota(jnp.int32, (depth, row_index.shape[1]), 0)
    return (rows == row_index).astype(jnp.float32).astype(jnp.bfloat16)


def merge_kernel(
    owners,
    step,
    order_ref,
    table_ref,
    own_ref,
    out_ref,
    joined,
    current,
    picks,
    first_pick,
    turned,
    halo_send,
    halo_recv,
    block_send,
    block_recv,
):
    levels, _, rows = table_ref.shape
    extra = step * (owners - 1)
    window = own_ref.shape[0]
    _, held, length = out_ref.shape
    whole = length + rows
    me = lax.axis_index("sub")

    barrier = pltpu.get_barrier_semaphore()
    for apart in range(1, owners):
        pl.semaphore_signal(
            barrier, inc=1, device_id={"sub": lax.rem(me + apart, owners)}, device_id_type=MESH
        )
    joined[extra : extra + window, :] = own_ref[...]
    first_pick[...] = one_hot(order_ref[...], order_ref.shape[1])
    pl.semaphore_wait(barrier, owners - 1)

    onward = pltpu.make_async_remote_copy(
        src_ref=own_ref.at[window - extra :],
        dst_ref=joined.at[0:extra],
        send_sem=halo_send.at[0],
        recv_sem=halo_recv.at[0],
        device_id={"sub": lax.rem(me + 1, owners)},
        device_id_type=MESH,
    )
    back = pltpu.make_async_remote_copy(
        src_ref=own_ref.at[0:extra],
        dst_ref=joined.at[extra + window :],
        send_sem=halo_send.at[1],
        recv_sem=halo_recv.at[1],
        device_id={"sub": lax.rem(me + owners - 1, owners)},
        device_id_type=MESH,
    )

    @pl.when(me < owners - 1)
    def _():
        onward.start()

    @pl.when(me > 0)
    def _():
        back.start()

    lanes = lax.broadcasted_iota(jnp.int32, (1, rows), 1)
    for level_num in range(2, levels + 1):
        child_rows = max(1, 2 ** (level_num - 2))
        entries = table_ref[level_num - 1]
        starts = 2 * child_rows * (lanes >> (level_num - 1))
        picks[level_num - 2, :, 0:rows] = one_hot(starts + entries[0:1], rows)
        picks[level_num - 2, :, rows:] = one_hot(starts + child_rows + entries[1:2], rows)

    @pl.when(me < owners - 1)
    def _():
        onward.wait_send()
        back.wait_recv()

    @pl.when(me > 0)
    def _():
        back.wait_send()
        onward.wait_recv()

    first = pl.multiple_of(extra - step * me, step)
    have = whole
    left = rows
    for level_num in range(1, levels + 1):
        child_rows = max(1, 2 ** (level_num - 2))
        shifts = table_ref[level_num - 1][2:3]
        if level_num == 1:
            chosen = first_pick[...]
            source = joined[pl.ds(first, whole), :]
        else:
            chosen = picks[level_num - 2]
            source = current[0:have, :]
        left -= child_rows
        keep = -(-(length + left) // 16) * 16
        picked = jnp.dot(source, chosen, preferred_element_type=jnp.float32)
        for base in range(0, rows, 128):
            moved = picked[:, rows + base : rows + base + 128]
            amounts = shifts[:, base : base + 128]
            for bit_num in reversed(range(child_rows.bit_length())):
                size = moved.shape[0]
                rolled = pltpu.roll(moved, size - 2**bit_num, axis=0)
                flagged = jnp.broadcast_to(amounts >> bit_num & 1, moved.shape) == 1
                moved = jnp.where(flagged, rolled, moved)
                needed = min(size, keep + -(-(2**bit_num - 1) // 8) * 8)
                moved = moved[0:needed]
            current[0:keep, base : base + 128] = (
                picked[0:keep, base : base + 128] + moved[0:keep]
            ).astype(jnp.bfloat16)
        have = keep
    places = lax.broadcasted_iota(jnp.int32, (rows, rows), 0)
    shift = held.bit_length() - 1
    sources = (reversed_bits(places >> shift, owners.bit_length() - 1) << shift) + (places & (held - 1))
    placed = (lax.broadcasted_iota(jnp.int32, (rows, rows), 1) == sources).astype(jnp.float32)
    turned[...] = lax.dot_general(
        placed.astype(jnp.bfloat16),
        current[0:length, :],
        (((1,), (1,)), ((), ())),
        preferred_element_type=jnp.float32,
    ).astype(jnp.bfloat16)

    copies = []
    for apart in range(1, owners):
        target = lax.rem(me + apart, owners)
        copy = pltpu.make_async_remote_copy(
            src_ref=turned.at[pl.ds(pl.multiple_of(target * held, held), held)],
            dst_ref=out_ref.at[me],
            send_sem=block_send.at[apart],
            recv_sem=block_recv.at[apart],
            device_id={"sub": target},
            device_id_type=MESH,
        )
        copy.start()
        copies.append(copy)
    out_ref[me] = turned[pl.ds(pl.multiple_of(me * held, held), held), :]
    for copy in copies:
        copy.wait()


def local_sliced(samples, channel_order, merge_table):
    owners = lax.axis_size("sub")
    window, channels = samples.shape
    levels, _, rows = merge_table.shape
    held = rows // owners
    length = window - held
    step = window - length
    extra = step * (owners - 1)
    order = channel_order.reshape(rows, 2).T.reshape(1, channels)
    vmem = pl.BlockSpec(memory_space=pltpu.VMEM)
    blocks = pl.pallas_call(
        functools.partial(merge_kernel, owners, step),
        out_shape=jax.ShapeDtypeStruct((owners, held, length), jnp.bfloat16),
        in_specs=[vmem] * 3,
        out_specs=vmem,
        scratch_shapes=[
            pltpu.VMEM((window + 2 * extra, channels), jnp.bfloat16),
            pltpu.VMEM((length + rows, rows), jnp.bfloat16),
            pltpu.VMEM((levels - 1, rows, 2 * rows), jnp.bfloat16),
            pltpu.VMEM((channels, channels), jnp.bfloat16),
            pltpu.VMEM((rows, length), jnp.bfloat16),
            pltpu.SemaphoreType.DMA((2,)),
            pltpu.SemaphoreType.DMA((2,)),
            pltpu.SemaphoreType.DMA((owners,)),
            pltpu.SemaphoreType.DMA((owners,)),
        ],
        compiler_params=pltpu.CompilerParams(
            vmem_limit_bytes=32 * 1024 * 1024, collective_id=0, has_side_effects=True
        ),
        name="merge_rows",
    )(order, merge_table, samples)
    series = blocks.transpose(1, 0, 2).reshape(held, owners * length)
    return spectrum(series, channels)


def is_sliced(window, owners, rows):
    step = rows // owners
    length = window - step
    return step % 16 == 0 and length % 128 == 0 and step * (owners - 1) <= window


def local_any(samples, channel_order, merge_table):
    if is_sliced(samples.shape[0], lax.axis_size("sub"), merge_table.shape[2]):
        return local_sliced(samples, channel_order, merge_table)
    return local(samples, channel_order, merge_table)


def solution(mesh):
    in_specs = (P(("groups", "sub"), None), P(), P())
    out_specs = P(("groups", "sub"), None)
    return jax.shard_map(local_any, mesh=mesh, in_specs=in_specs, out_specs=out_specs, check_vma=False)
```

```python
import functools
import math

import jax
import jax.numpy as jnp
from jax import lax
from jax.experimental import pallas as pl
from jax.experimental.pallas import tpu as pltpu
from jax.sharding import PartitionSpec as P

LOCAL = 5
MESH = pl.DeviceIdType.MESH
CH_DEV = 32
SAMPLES = 8192


def from_partner(block, axis, apart):
    count = lax.axis_size(axis)
    route = []
    for low in range(count):
        high = low | 1 << apart
        if high != low and high < count:
            route += [(low, high), (high, low)]
    return lax.ppermute(block, axis, route)


def delay_rows(values, shifts, margin, time_axis):
    length = values.shape[time_axis]
    moved = values
    for bit_num in range(max(1, margin.bit_length())):
        offset = 2**bit_num
        rolled = jnp.pad(moved[:, offset:], ((0, 0), (0, offset)))
        flagged = shifts >> bit_num & 1 == 1
        flagged = flagged[:, None]
        moved = jnp.where(flagged, rolled, moved)
    return moved


def merge_level(current, entries, child_rows, span_rows, time_axis):
    outputs = jnp.arange(entries.shape[1], dtype=jnp.int32)
    starts = 2 * child_rows * (outputs // span_rows)
    lower_rows = jnp.take(current, starts + entries[0], axis=1 - time_axis)
    upper_rows = jnp.take(current, starts + child_rows + entries[1], axis=1 - time_axis)
    moved_rows = delay_rows(upper_rows, entries[2], child_rows, time_axis)
    return (lower_rows.astype(jnp.float32) + moved_rows.astype(jnp.float32)).astype(jnp.bfloat16)


def spectrum(delays, channels):
    row_count = delays.shape[0]
    length = delays.shape[1]
    fold_size = length // 128
    first_index = jnp.arange(fold_size, dtype=jnp.int32)
    lane_index = jnp.arange(128, dtype=jnp.int32)
    half_index = jnp.arange(64, dtype=jnp.int32)
    angle_one = (
        2.0
        * math.pi
        / fold_size
        * (first_index[:, None] * first_index[None, :] % fold_size).astype(jnp.float32)
    )
    cos_one = jnp.cos(angle_one).astype(jnp.bfloat16)
    sin_one = jnp.sin(angle_one).astype(jnp.bfloat16)
    angle_two = (
        2.0
        * math.pi
        / length
        * (first_index[:, None] * lane_index[None, :] % length).astype(jnp.float32)
    )
    twist_cos = jnp.cos(angle_two)
    twist_sin = jnp.sin(angle_two)
    angle_three = (
        2.0 * math.pi / 128 * (lane_index[:, None] * half_index[None, :] % 128).astype(jnp.float32)
    )
    cos_three = jnp.cos(angle_three).astype(jnp.bfloat16)
    sin_three = jnp.sin(angle_three).astype(jnp.bfloat16)
    series = delays.reshape(row_count, fold_size, 128)
    first_re = jnp.einsum("kn,rnm->rkm", cos_one, series, preferred_element_type=jnp.float32)
    first_im = -jnp.einsum("kn,rnm->rkm", sin_one, series, preferred_element_type=jnp.float32)
    twisted_re = (first_re * twist_cos + first_im * twist_sin).astype(jnp.bfloat16)
    twisted_im = (first_im * twist_cos - first_re * twist_sin).astype(jnp.bfloat16)
    out_re = jnp.einsum(
        "rkn,nj->rjk", twisted_re, cos_three, preferred_element_type=jnp.float32
    ) + jnp.einsum("rkn,nj->rjk", twisted_im, sin_three, preferred_element_type=jnp.float32)
    out_im = jnp.einsum(
        "rkn,nj->rjk", twisted_im, cos_three, preferred_element_type=jnp.float32
    ) - jnp.einsum("rkn,nj->rjk", twisted_re, sin_three, preferred_element_type=jnp.float32)
    power = (out_re * out_re + out_im * out_im) / (length * channels)
    return power.reshape(row_count, 64 * fold_size)


def local(samples, channel_order, merge_table):
    owners = lax.axis_size("sub")
    owner_index = lax.axis_index("sub")
    owned_rows = CH_DEV // 2
    quarter = CH_DEV // 4
    window = samples.shape[0]
    channels = samples.shape[1]
    ordered = jnp.take(samples, channel_order, axis=1).T.reshape(owners, CH_DEV, window)
    current = lax.all_to_all(ordered, "sub", split_axis=0, concat_axis=2, tiled=True).reshape(
        CH_DEV, window * owners
    )
    for level_num in range(1, LOCAL + 1):
        entries = lax.dynamic_slice_in_dim(
            merge_table[level_num - 1], owner_index * owned_rows, owned_rows, 1
        )
        current = merge_level(
            current, entries, max(1, 2 ** (level_num - 2)), 2 ** (level_num - 1), 1
        )
    block_index = jnp.zeros((), jnp.int32)
    for bit_num in range(owners.bit_length() - 1):
        level_num = LOCAL + bit_num + 1
        half_bit = owner_index >> bit_num & 1
        block_index = block_index * 2 + half_bit
        span_rows = owned_rows * 2 ** (bit_num + 1)
        child_rows = span_rows // 2
        subband = owner_index >> bit_num + 1
        entries = lax.dynamic_slice_in_dim(
            merge_table[level_num - 1],
            subband * span_rows + owned_rows * block_index,
            owned_rows,
            1,
        )
        kept_rows = lax.dynamic_slice_in_dim(current, half_bit * quarter, quarter, 0)
        sent_rows = lax.dynamic_slice_in_dim(current, (1 - half_bit) * quarter, quarter, 0)
        partner = from_partner(sent_rows, "sub", bit_num)
        row_base = quarter * block_index
        is_low = half_bit == 0
        lower_part = jnp.where(is_low, kept_rows, partner)
        upper_part = jnp.where(is_low, partner, kept_rows)
        lower_rows = jnp.take(lower_part, entries[0] - row_base, axis=0)
        upper_rows = jnp.take(upper_part, entries[1] - row_base, axis=0)
        moved_rows = delay_rows(upper_rows, entries[2], child_rows, 1)
        current = (lower_rows.astype(jnp.float32) + moved_rows.astype(jnp.float32)).astype(
            jnp.bfloat16
        )
    return spectrum(current[:, :SAMPLES], channels)


def reversed_bits(values, bits):
    flipped = jnp.zeros_like(values)
    for bit_num in range(bits):
        flipped = flipped | ((values >> bit_num & 1) << (bits - 1 - bit_num))
    return flipped


def one_hot(row_index, depth):
    rows = lax.broadcasted_iota(jnp.int32, (depth, row_index.shape[1]), 0)
    return (rows == row_index).astype(jnp.float32).astype(jnp.bfloat16)


def merge_kernel(
    owners,
    step,
    order_hbm,
    table_hbm,
    own_ref,
    out_ref,
    order_ref,
    table_ref,
    joined,
    current,
    picks,
    first_pick,
    turned,
    halo_send,
    halo_recv,
    block_send,
    block_recv,
    load_sem,
):
    levels, _, rows = table_ref.shape
    extra = step * (owners - 1)
    window = own_ref.shape[0]
    _, held, length = out_ref.shape
    whole = length + rows
    me = lax.axis_index("sub")

    loads = [
        pltpu.make_async_copy(order_hbm, order_ref, load_sem.at[0]),
        pltpu.make_async_copy(table_hbm, table_ref, load_sem.at[1]),
        pltpu.make_async_copy(own_ref, joined.at[extra : extra + window], load_sem.at[2]),
    ]
    for load in loads:
        load.start()
    barrier = pltpu.get_barrier_semaphore()
    for apart in range(1, owners):
        pl.semaphore_signal(
            barrier, inc=1, device_id={"sub": lax.rem(me + apart, owners)}, device_id_type=MESH
        )
    loads[0].wait()
    channels = order_ref.shape[1]
    column = lax.broadcasted_iota(jnp.int32, (1, channels), 1)
    split = jnp.where(column < rows, 2 * column, 2 * (column - rows) + 1)
    first_pick[...] = jnp.dot(
        one_hot(order_ref[...], channels),
        one_hot(split, channels),
        preferred_element_type=jnp.float32,
    ).astype(jnp.bfloat16)
    pl.semaphore_wait(barrier, owners - 1)

    onward = pltpu.make_async_remote_copy(
        src_ref=own_ref.at[window - extra :],
        dst_ref=joined.at[0:extra],
        send_sem=halo_send.at[0],
        recv_sem=halo_recv.at[0],
        device_id={"sub": lax.rem(me + 1, owners)},
        device_id_type=MESH,
    )
    back = pltpu.make_async_remote_copy(
        src_ref=own_ref.at[0:extra],
        dst_ref=joined.at[extra + window :],
        send_sem=halo_send.at[1],
        recv_sem=halo_recv.at[1],
        device_id={"sub": lax.rem(me + owners - 1, owners)},
        device_id_type=MESH,
    )

    @pl.when(me < owners - 1)
    def _():
        onward.start()

    @pl.when(me > 0)
    def _():
        back.start()

    loads[1].wait()
    lanes = lax.broadcasted_iota(jnp.int32, (1, rows), 1)
    for level_num in range(2, levels + 1):
        child_rows = max(1, 2 ** (level_num - 2))
        entries = table_ref[level_num - 1]
        starts = 2 * child_rows * (lanes >> (level_num - 1))
        picks[level_num - 2, :, 0:rows] = one_hot(starts + entries[0:1], rows)
        picks[level_num - 2, :, rows:] = one_hot(starts + child_rows + entries[1:2], rows)

    @pl.when(me < owners - 1)
    def _():
        onward.wait_send()
        back.wait_recv()

    @pl.when(me > 0)
    def _():
        back.wait_send()
        onward.wait_recv()

    loads[2].wait()
    first = pl.multiple_of(extra - step * me, step)
    have = whole
    left = rows
    for level_num in range(1, levels + 1):
        child_rows = max(1, 2 ** (level_num - 2))
        shifts = table_ref[level_num - 1][2:3]
        if level_num == 1:
            chosen = first_pick[...]
            source = joined[pl.ds(first, whole), :]
        else:
            chosen = picks[level_num - 2]
            source = current[0:have, :]
        left -= child_rows
        keep = -(-(length + left) // 16) * 16
        picked = jnp.dot(source, chosen, preferred_element_type=jnp.float32)
        for base in range(0, rows, 128):
            moved = picked[:, rows + base : rows + base + 128]
            amounts = shifts[:, base : base + 128]
            for bit_num in reversed(range(child_rows.bit_length())):
                size = moved.shape[0]
                rolled = pltpu.roll(moved, size - 2**bit_num, axis=0)
                flagged = jnp.broadcast_to(amounts >> bit_num & 1, moved.shape) == 1
                moved = jnp.where(flagged, rolled, moved)
                needed = min(size, keep + -(-(2**bit_num - 1) // 8) * 8)
                moved = moved[0:needed]
            current[0:keep, base : base + 128] = (
                picked[0:keep, base : base + 128] + moved[0:keep]
            ).astype(jnp.bfloat16)
        have = keep
    places = lax.broadcasted_iota(jnp.int32, (rows, rows), 0)
    shift = held.bit_length() - 1
    sources = (reversed_bits(places >> shift, owners.bit_length() - 1) << shift) + (places & (held - 1))
    placed = (lax.broadcasted_iota(jnp.int32, (rows, rows), 1) == sources).astype(jnp.float32)
    turned[...] = lax.dot_general(
        placed.astype(jnp.bfloat16),
        current[0:length, :],
        (((1,), (1,)), ((), ())),
        preferred_element_type=jnp.float32,
    ).astype(jnp.bfloat16)

    copies = []
    for apart in range(1, owners):
        target = lax.rem(me + apart, owners)
        copy = pltpu.make_async_remote_copy(
            src_ref=turned.at[pl.ds(pl.multiple_of(target * held, held), held)],
            dst_ref=out_ref.at[me],
            send_sem=block_send.at[apart],
            recv_sem=block_recv.at[apart],
            device_id={"sub": target},
            device_id_type=MESH,
        )
        copy.start()
        copies.append(copy)
    out_ref[me] = turned[pl.ds(pl.multiple_of(me * held, held), held), :]
    for copy in copies:
        copy.wait()


def local_sliced(samples, channel_order, merge_table):
    owners = lax.axis_size("sub")
    window, channels = samples.shape
    levels, _, rows = merge_table.shape
    held = rows // owners
    length = window - held
    step = window - length
    extra = step * (owners - 1)
    order = channel_order.reshape(1, channels)
    vmem = pl.BlockSpec(memory_space=pltpu.VMEM)
    blocks = pl.pallas_call(
        functools.partial(merge_kernel, owners, step),
        out_shape=jax.ShapeDtypeStruct((owners, held, length), jnp.bfloat16),
        in_specs=[pl.BlockSpec(memory_space=pl.ANY)] * 3,
        out_specs=vmem,
        scratch_shapes=[
            pltpu.VMEM((1, channels), jnp.int32),
            pltpu.VMEM((levels, 3, rows), jnp.int32),
            pltpu.VMEM((window + 2 * extra, channels), jnp.bfloat16),
            pltpu.VMEM((length + rows, rows), jnp.bfloat16),
            pltpu.VMEM((levels - 1, rows, 2 * rows), jnp.bfloat16),
            pltpu.VMEM((channels, channels), jnp.bfloat16),
            pltpu.VMEM((rows, length), jnp.bfloat16),
            pltpu.SemaphoreType.DMA((2,)),
            pltpu.SemaphoreType.DMA((2,)),
            pltpu.SemaphoreType.DMA((owners,)),
            pltpu.SemaphoreType.DMA((owners,)),
            pltpu.SemaphoreType.DMA((3,)),
        ],
        compiler_params=pltpu.CompilerParams(
            vmem_limit_bytes=62 * 1024 * 1024, collective_id=0, has_side_effects=True
        ),
        name="merge_rows",
    )(order, merge_table, samples)
    series = blocks.transpose(1, 0, 2).reshape(held, owners * length)
    return spectrum(series, channels)


def is_sliced(window, owners, rows):
    step = rows // owners
    length = window - step
    return step % 16 == 0 and length % 128 == 0 and step * (owners - 1) <= window


def local_any(samples, channel_order, merge_table):
    if is_sliced(samples.shape[0], lax.axis_size("sub"), merge_table.shape[2]):
        return local_sliced(samples, channel_order, merge_table)
    return local(samples, channel_order, merge_table)


def solution(mesh):
    in_specs = (P(("groups", "sub"), None), P(), P())
    out_specs = P(("groups", "sub"), None)
    return jax.shard_map(local_any, mesh=mesh, in_specs=in_specs, out_specs=out_specs, check_vma=False)
```
